32 devices in a mesh: blk: 8 (over z, y), grp: 4 (over x, core).
Axes of the slice: x: 2, y: 2, z: 4, core: 2. Of those that a mesh axis runs over, the one named last changes fastest.
Arguments:
- hidden: bfloat16 [65536, 384], P(('blk', 'grp')), may hold values from -6 to 6
- cotangent: bfloat16 [65536, 384], P(('blk', 'grp')), may hold values from -6 to 6
- token_ids: int32 [65536], P(('blk', 'grp')), may hold values from 0 to 32127, as said below
- w_in: bfloat16 [8, 4, 384, 1536], P('blk', 'grp'), may hold values from -6 to 6
- w_out: bfloat16 [1536, 384], replicated, may hold values from -0.15625 to 0.15625
- tracker: bfloat16 [8, 4, 384, 1536], P('blk', 'grp'), may hold values from -6 to 6
- grad_old: bfloat16 [8, 4, 384, 1536], P('blk', 'grp'), may hold values from -6 to 6
- cheb_num: int32 [4], replicated, may hold values from 10 to 16
- cheb_den: int32 [4], replicated, may hold values from 9 to 11
Outputs:
- new_params: bfloat16 [8, 4, 384, 1536], P('blk', 'grp')
- new_tracker: bfloat16 [8, 4, 384, 1536], P('blk', 'grp')
The draws below stay inside these ranges and needn't reach their ends.
Inputs may be any that keep to these rules, and one draw needn't show every extreme that they name: `token_ids`: each aligned run of 512 rows is one sequence: ids from 1 to 32127 up to its length, 0 after it; every length is 128 or more.
All inputs are finite; a program needn't handle non-finite values.
Results may differ from the reference program's by a relative error of at most 0.013.
Values may be sent and summed in bfloat16 or wider, within the bound.
A program may use at most 128 MiB of HBM per device.

```python
import math
import jax
import jax.numpy as jnp
from jax import lax

D = 384
FF = 1536
VOCAB = 32128
SEQ_LEN = 512
ROUNDS = 4
TOK_DEV = 2048
TOKENS = 65536
N_BLK = 8
N_GRP = 4


def draw_token_ids(key, part):
    base_key = jax.random.fold_in(key, 7)
    length_key, value_key = jax.random.split(base_key)
    count = TOKENS // SEQ_LEN
    lengths = jax.random.randint(length_key, (count, 1), SEQ_LEN // 4, SEQ_LEN + 1)
    values = jax.random.randint(value_key, (count, SEQ_LEN), 1, VOCAB)
    position = jnp.arange(SEQ_LEN, dtype=jnp.int32)[None, :]
    return jnp.where(position < lengths, values, 0).astype(jnp.int32).reshape(TOKENS)


def with_ends(entries, stream_key, low, largest):
    place = [jax.random.randint(jax.random.fold_in(stream_key, axis), (), 0, length) for axis, length in enumerate(entries.shape)]
    widest = entries.shape.index(max(entries.shape))
    next_to = place[:widest] + [(place[widest] + 1) % entries.shape[widest]] + place[widest + 1:]
    return entries.at[tuple(place)].set(low).at[tuple(next_to)].set(largest)


def levels(rng, shape, cuts, least, largest):
    def one(dim, blocks):
        heights = jax.random.uniform(jax.random.fold_in(jax.random.fold_in(rng, 6), dim), (blocks,), jnp.float32, least / len(cuts), largest / len(cuts))
        return jnp.repeat(jnp.exp(heights), shape[dim] // blocks).reshape((-1,) + (1,) * (len(shape) - dim - 1))

    factor_of = one(*cuts[0])
    for cut in cuts[1:]:
        factor_of = factor_of * one(*cut)
    return factor_of


def normal_values(key, extent, deviation, bound, cuts=(), held_as=jnp.bfloat16):
    values = jax.random.normal(key, extent, jnp.float32) * deviation
    if len(cuts) > 0:
        values = levels(key, extent, cuts, -0.22, 0.18) * values
    return jnp.clip(values, min=-bound, max=bound).astype(held_as)


def setup_inputs(seed: int = 0) -> dict:
    arg_keys = jax.random.split(jax.random.key(seed), 10)
    return {
        "hidden": normal_values(arg_keys[0], (TOKENS, D), 1.0, 6.0, ((0, 32),)),
        "cotangent": normal_values(arg_keys[1], (TOKENS, D), 1.0, 6.0, ((0, 32),)),
        "token_ids": draw_token_ids(jax.random.fold_in(arg_keys[9], 71), 0),
        "w_in": normal_values(arg_keys[3], (N_BLK, N_GRP, D, FF), 1.0, 6.0, ((0, 8), (1, 4))),
        "w_out": normal_values(arg_keys[4], (FF, D), FF ** -0.5, 0.15625),
        "tracker": normal_values(arg_keys[5], (N_BLK, N_GRP, D, FF), 0.5, 6.0, ((0, 8), (1, 4))),
        "grad_old": normal_values(arg_keys[6], (N_BLK, N_GRP, D, FF), 0.5, 6.0, ((0, 8), (1, 4))),
        "cheb_num": with_ends(jax.random.randint(arg_keys[7], (ROUNDS,), 10, 17), jax.random.fold_in(arg_keys[7], 1), 10, 16).astype(jnp.int32),
        "cheb_den": with_ends(jax.random.randint(arg_keys[8], (ROUNDS,), 9, 12), jax.random.fold_in(arg_keys[8], 1), 9, 11).astype(jnp.int32),
    }


epsilon = 1e-06
step_size = 0.25
tanh_scale = math.sqrt(2.0 / math.pi)

def gelu_slope(values):
    cubic = values * values * values
    bent_tanh = jnp.tanh(tanh_scale * (values + 0.044715 * cubic))
    return 0.5 * (1.0 + bent_tanh) + 0.5 * values * (1.0 - bent_tanh * bent_tanh) * tanh_scale * (1.0 + 3.0 * 0.044715 * values * values)

def cycle(field):
    return (jnp.roll(field, 1, 0) + field + jnp.roll(field, -1, 0)) / 3.0

def local_grad(packed, w_out):
    rows, grads_in, ids_rows, params = packed
    widened = rows.astype(jnp.float32)
    mean_square = lax.optimization_barrier(jnp.mean(widened * widened, axis=-1, keepdims=True))
    normed = (widened * lax.rsqrt(mean_square + epsilon)).astype(jnp.bfloat16)
    inv_root = params.shape[0] ** (-0.5)
    pre_act = jnp.dot(normed, params, preferred_element_type=jnp.float32) * inv_root
    masked = jnp.where((ids_rows != 0)[:, None], grads_in, jnp.zeros_like(grads_in))
    back_flow = lax.dot_general(masked, w_out, (((1,), (1,)), ((), ())), preferred_element_type=jnp.float32)
    slope_bf = (back_flow * gelu_slope(pre_act)).astype(jnp.bfloat16)
    return lax.dot_general(normed, slope_bf, (((0,), (0,)), ((), ())), preferred_element_type=jnp.float32) * inv_root

def reference(hidden, cotangent, token_ids, w_in, w_out, tracker, grad_old, cheb_num, cheb_den):
    cycle_mixed = cycle(w_in.astype(jnp.float32))
    mixed_params = lax.optimization_barrier(jnp.sum(cycle_mixed, axis=1, keepdims=True)) / N_GRP
    new_params = (mixed_params - step_size * tracker.astype(jnp.float32)).astype(jnp.bfloat16)
    weights = cheb_num.astype(jnp.float32) / cheb_den.astype(jnp.float32)
    older_iter = tracker.astype(jnp.float32)
    current = older_iter
    for turn_idx in range(ROUNDS):
        next_iter = weights[turn_idx] * cycle(current) + (1.0 - weights[turn_idx]) * older_iter
        older_iter, current = (current, next_iter)
    workers = N_BLK * N_GRP
    packed = (hidden.reshape(workers, TOK_DEV, D), cotangent.reshape(workers, TOK_DEV, D), token_ids.reshape(workers, TOK_DEV), new_params.reshape(workers, D, FF))
    grad_new = lax.map(lambda item: local_grad(item, w_out), packed).reshape(N_BLK, N_GRP, D, FF)
    new_tracker = (current + grad_new - grad_old.astype(jnp.float32)).astype(jnp.bfloat16)
    return (new_params, new_tracker)
```

```python
import functools
import math

import jax
import jax.numpy as jnp
from jax import lax
from jax.experimental import pallas as pl
from jax.experimental.pallas import tpu as pltpu
from jax.sharding import PartitionSpec as P

ROUNDS = 4


epsilon = 1e-06
step_size = 0.25
tanh_scale = math.sqrt(2.0 / math.pi)


def padded(cells, sides, width):
    for axis, dim in sides:
        count = lax.axis_size(axis)
        head = lax.slice_in_dim(cells, 0, width, axis=dim)
        tail = lax.slice_in_dim(cells, cells.shape[dim] - width, cells.shape[dim], axis=dim)
        cells = jnp.concatenate(
            [
                lax.ppermute(tail, axis, [(i, (i + 1) % count) for i in range(count)]),
                cells,
                lax.ppermute(head, axis, [((i + 1) % count, i) for i in range(count)]),
            ],
            axis=dim,
        )
    return cells


def passed_along(value, axis, by):
    devices = lax.axis_size(axis)
    return lax.ppermute(value, axis, [(i, (i + by) % devices) for i in range(devices)])


def gelu_slope(values):
    cubic = values * values * values
    bent_tanh = jnp.tanh(tanh_scale * (values + 0.044715 * cubic))
    return 0.5 * (1.0 + bent_tanh) + 0.5 * values * (1.0 - bent_tanh * bent_tanh) * tanh_scale * (
        1.0 + 3.0 * 0.044715 * values * values
    )


def cycle_mean(beside_all):
    return ((beside_all[0] + beside_all[1] + beside_all[2]) / 3.0)[None]


def local_grad(hidden, cotangent, token_ids, params, w_out):
    widened = hidden.astype(jnp.float32)
    mean_square = jnp.mean(widened * widened, axis=-1, keepdims=True)
    normed = (widened * lax.rsqrt(mean_square + epsilon)).astype(jnp.bfloat16)
    inv_root = params.shape[0] ** (-0.5)
    pre_act = jnp.dot(normed, params, preferred_element_type=jnp.float32) * inv_root
    masked = jnp.where((token_ids != 0)[:, None], cotangent, jnp.zeros_like(cotangent))
    back_flow = lax.dot_general(
        masked, w_out, (((1,), (1,)), ((), ())), preferred_element_type=jnp.float32
    )
    slope_bf = (back_flow * gelu_slope(pre_act)).astype(jnp.bfloat16)
    return (
        lax.dot_general(
            normed, slope_bf, (((0,), (0,)), ((), ())), preferred_element_type=jnp.float32
        )
        * inv_root
    )


def shards(hidden, cotangent, token_ids, w_in, w_out, tracker, grad_old, cheb_num, cheb_den):
    beside_all = padded(w_in, (("blk", 0),), 1).astype(jnp.float32)
    cycle_mixed = cycle_mean(beside_all)
    groups = lax.axis_size("grp")
    group_sum = lax.psum(cycle_mixed.astype(jnp.bfloat16), "grp").astype(jnp.float32)
    group_avg = group_sum / groups
    new_params = (group_avg - step_size * tracker.astype(jnp.float32)).astype(jnp.bfloat16)
    weights = cheb_num.astype(jnp.float32) / cheb_den.astype(jnp.float32)
    start_iter = tracker.astype(jnp.float32)
    coeffs = jnp.zeros((2 * ROUNDS + 1,), jnp.float32).at[ROUNDS].set(1.0)
    older_coef = coeffs
    current_coef = coeffs
    for turn_idx in range(ROUNDS):
        mixed_coef = (jnp.roll(current_coef, 1) + current_coef + jnp.roll(current_coef, -1)) / 3.0
        next_coef = weights[turn_idx] * mixed_coef + (1.0 - weights[turn_idx]) * older_coef
        older_coef, current_coef = (current_coef, next_coef)
    consensus = current_coef[ROUNDS] * start_iter
    for hop_len in range(1, ROUNDS + 1):
        for direction in (1, -1):
            shifted = passed_along(tracker, "blk", direction * hop_len)
            consensus = consensus + current_coef[ROUNDS + direction * hop_len] * shifted.astype(
                jnp.float32
            )
    grad_new = local_grad(hidden, cotangent, token_ids, new_params[0, 0], w_out)[None, None]
    new_tracker = (consensus + grad_new - grad_old.astype(jnp.float32)).astype(jnp.bfloat16)
    return (new_params, new_tracker)


MESH = pl.DeviceIdType.MESH
f32 = jnp.float32
bf16 = jnp.bfloat16


def cycle_coeffs(num_ref, den_ref, count):
    coef = [1.0] + [0.0] * (ROUNDS + 1)
    older = coef
    for turn in range(ROUNDS):
        omega = jnp.full((1, 128), num_ref[turn], jnp.int32).astype(f32) / jnp.full(
            (1, 128), den_ref[turn], jnp.int32
        ).astype(f32)
        following = []
        for dist in range(ROUNDS + 1):
            mixed = (coef[abs(dist - 1)] + coef[dist] + coef[dist + 1]) / 3.0
            following.append(omega * mixed + (1.0 - omega) * older[dist])
        older, coef = (coef, following + [0.0])
    folded = [None] * count
    for hop in range(-ROUNDS, ROUNDS + 1):
        at = hop % count
        folded[at] = coef[abs(hop)] if folded[at] is None else folded[at] + coef[abs(hop)]
    return folded


def fused_kernel(
    n, groups, tile,
    num_ref, den_ref, ids_ref, hid_ref, cot_ref, win_ref, wout_ref, trk_ref, old_ref,
    par_out, trk_out,
    hid, cot, win, wout, trk, old,
    wout_t, normed, normed_t, back, slope, grad,
    rs_core, rs_send, rs_x, m_own, m_bf, m_recv, mix, params,
    got, cons_send, cons, result,
    load_sem, core_s, core_r, x_s, x_r, nb_s, nb_r, ag_s, ag_r, p1_s, p1_r, p2_s, p2_r,
    po_sem, to_sem,
):
    b = lax.axis_index("blk")
    g = lax.axis_index("grp")
    rows_all, depth = hid.shape
    width = win.shape[1]
    part = width // groups
    chunk = depth // n
    core, side = lax.rem(g, 2), g // 2
    core_peer = side * 2 + (1 - core)
    x_peer = (1 - side) * 2 + core
    diag = (1 - side) * 2 + (1 - core)
    inv_root = depth ** (-0.5)

    def cols(which):
        return pl.ds(pl.multiple_of(which * part, 128), part)

    def rows(which):
        return pl.ds(pl.multiple_of(which * chunk, 16), chunk)

    def ring(by):
        return lax.rem(b + (by + n), n)

    loads = [
        pltpu.make_async_copy(s, d, load_sem.at[i])
        for i, (s, d) in enumerate(
            [(wout_ref, wout), (hid_ref, hid), (cot_ref, cot), (win_ref, win), (trk_ref, trk), (old_ref, old)]
        )
    ]
    for load in loads:
        load.start()

    barrier = pltpu.get_barrier_semaphore()
    for peer in (core_peer, x_peer):
        pl.semaphore_signal(barrier, inc=1, device_id=(b, peer), device_id_type=MESH)
    for by in range(1, n):
        pl.semaphore_signal(barrier, inc=1, device_id=(ring(by), g), device_id_type=MESH)
    pl.semaphore_wait(barrier, n + 1)

    def remote(source, target, send, recv, to):
        return pltpu.make_async_remote_copy(
            src_ref=source, dst_ref=target, send_sem=send, recv_sem=recv,
            device_id=to, device_id_type=MESH,
        )

    to_core = [
        remote(win_ref.at[:, cols(w)], rs_core.at[i], core_s.at[i], core_r.at[i], (b, core_peer))
        for i, w in ((1, diag), (0, core_peer))
    ]
    for copy in to_core:
        copy.start()
    first = {
        by: remote(
            trk_ref.at[rows(ring(by))], got.at[by], p1_s.at[by], p1_r.at[by], (ring(by), g)
        )
        for by in range(1, n)
    }
    order = sorted(range(1, n), key=lambda by: -min(by, n - by))
    for by in order:
        first[by].start()

    loads[0].wait()
    wout_t[...] = wout[...].T
    loads[2].wait()

    def flow(i, carry):
        at = pl.ds(pl.multiple_of(i * tile, tile), tile)
        back[at, :] = jnp.dot(cot[at, :], wout_t[...], preferred_element_type=f32)
        return carry

    loads[1].wait()

    def norm(i, carry):
        at = pl.ds(pl.multiple_of(i * tile, tile), tile)
        wide = hid[at, :].astype(f32)
        mean_square = jnp.mean(wide * wide, axis=-1, keepdims=True)
        scaled = (wide * lax.rsqrt(mean_square + epsilon)).astype(bf16)
        normed[at, :] = scaled
        flipped = scaled.astype(f32).T
        normed_t[:, at] = jnp.where(ids_ref[:, at] != 0, flipped, 0.0).astype(bf16)
        return carry

    loads[3].wait()
    for copy in to_core:
        copy.wait()
    rs_send[...] = (win[:, cols(x_peer)].astype(f32) + rs_core[1].astype(f32)).astype(bf16)
    to_x = remote(rs_send, rs_x, x_s.at[0], x_r.at[0], (b, x_peer))
    to_x.start()
    m_own[...] = win[:, cols(g)].astype(f32) + rs_core[0].astype(f32)
    lax.fori_loop(0, rows_all // tile, norm, 0)
    to_x.wait()
    m_own[...] += rs_x[...].astype(f32)
    m_bf[...] = m_own[...].astype(bf16)
    beside = [
        remote(m_bf, m_recv.at[i], nb_s.at[i], nb_r.at[i], (ring(by), g))
        for i, by in ((0, 1), (1, -1))
    ]
    for copy in beside:
        copy.start()
    lax.fori_loop(0, rows_all // tile, flow, 0)

    loads[4].wait()
    loads[5].wait()
    for by in order:
        first[by].wait()
    got[0] = trk[rows(b), :]
    coef = cycle_coeffs(num_ref, den_ref, n)
    lanes = coef[0].shape[1]

    def combine(i, carry):
        at = pl.ds(pl.multiple_of(i * lanes, lanes), lanes)
        parts = [got[by, :, at].astype(f32) for by in range(n)]
        for to in range(n):
            total = coef[to] * parts[0]
            for by in range(1, n):
                total = total + coef[(to + by) % n] * parts[by]
            if to == 0:
                cons[rows(b), at] = total.astype(bf16)
            else:
                cons_send[to, :, at] = total.astype(bf16)
        return carry

    lax.fori_loop(0, width // lanes, combine, 0)
    second = {
        by: remote(cons_send.at[by], cons.at[rows(b)], p2_s.at[by], p2_r.at[by], (ring(by), g))
        for by in range(1, n)
    }
    for by in order:
        second[by].start()

    for copy in beside:
        copy.wait()
    mix[0] = (
        (m_own[...] + m_recv[0].astype(f32) + m_recv[1].astype(f32)) / (3.0 * groups)
    ).astype(bf16)
    gather = [
        remote(mix.at[0], mix.at[1], ag_s.at[0], ag_r.at[0], (b, x_peer)),
        remote(mix.at[0], mix.at[2], ag_s.at[1], ag_r.at[1], (b, core_peer)),
        remote(mix.at[1], mix.at[3], ag_s.at[2], ag_r.at[2], (b, core_peer)),
    ]
    gather[0].start()
    gather[1].start()

    written = []
    for slot, owner in ((0, g), (2, core_peer), (1, x_peer), (3, diag)):
        if slot == 2:
            gather[1].wait()
        if slot == 1:
            gather[0].wait()
            gather[2].start()
        if slot == 3:
            gather[2].wait()
        here = cols(owner)
        params[slot] = (
            mix[slot].astype(f32) - step_size * trk[:, here].astype(f32)
        ).astype(bf16)
        copy = pltpu.make_async_copy(params.at[slot], par_out.at[:, here], po_sem.at[slot])
        copy.start()
        written.append(copy)

        def tokens(i, carry, slot=slot, here=here):
            at = pl.ds(pl.multiple_of(i * tile, tile), tile)
            p = jnp.dot(normed[at, :], params[slot], preferred_element_type=f32) * inv_root
            square = p * p
            bent = jnp.tanh(p * (tanh_scale + (tanh_scale * 0.044715) * square))
            ramp = p * (tanh_scale + (3.0 * 0.044715 * tanh_scale) * square)
            bend = (1.0 + bent) * (1.0 + (1.0 - bent) * ramp)
            slope[at, :] = (back[at, here] * (0.5 * bend)).astype(bf16)
            return carry

        lax.fori_loop(0, rows_all // tile, tokens, 0)
        grad[:, here] = (
            jnp.dot(normed_t[...], slope[...], preferred_element_type=f32) * inv_root
            - old[:, here].astype(f32)
        )

    for by in [0] + order:
        if by:
            second[by].wait()
        here = rows(ring(-by))
        result[here, :] = (grad[here, :] + cons[here, :].astype(f32)).astype(bf16)
        copy = pltpu.make_async_copy(result.at[here], trk_out.at[here], to_sem.at[by])
        copy.start()
        written.append(copy)
    for copy in written:
        copy.wait()


def fused_shards(hidden, cotangent, token_ids, w_in, w_out, tracker, grad_old, cheb_num, cheb_den):
    n, groups = lax.axis_size("blk"), lax.axis_size("grp")
    tokens, depth = hidden.shape
    width = w_in.shape[-1]
    part, chunk = width // groups, depth // n
    tile = 256
    leaf = jax.ShapeDtypeStruct((depth, width), bf16)
    hbm, smem, vmem = (
        pl.BlockSpec(memory_space=space) for space in (pl.ANY, pltpu.SMEM, pltpu.VMEM)
    )
    dma = pltpu.SemaphoreType.DMA
    new_params, new_tracker = pl.pallas_call(
        functools.partial(fused_kernel, n, groups, tile),
        out_shape=(leaf, leaf),
        in_specs=[smem, smem, vmem] + [hbm] * 6,
        out_specs=(hbm, hbm),
        scratch_shapes=[
            pltpu.VMEM((tokens, depth), bf16),
            pltpu.VMEM((tokens, depth), bf16),
            pltpu.VMEM((depth, width), bf16),
            pltpu.VMEM((width, depth), bf16),
            pltpu.VMEM((depth, width), bf16),
            pltpu.VMEM((depth, width), bf16),
            pltpu.VMEM((depth, width), bf16),
            pltpu.VMEM((tokens, depth), bf16),
            pltpu.VMEM((depth, tokens), bf16),
            pltpu.VMEM((tokens, width), f32),
            pltpu.VMEM((tokens, part), bf16),
            pltpu.VMEM((depth, width), f32),
            pltpu.VMEM((2, depth, part), bf16),
            pltpu.VMEM((depth, part), bf16),
            pltpu.VMEM((depth, part), bf16),
            pltpu.VMEM((depth, part), f32),
            pltpu.VMEM((depth, part), bf16),
            pltpu.VMEM((2, depth, part), bf16),
            pltpu.VMEM((4, depth, part), bf16),
            pltpu.VMEM((4, depth, part), bf16),
            pltpu.VMEM((n, chunk, width), bf16),
            pltpu.VMEM((n, chunk, width), bf16),
            pltpu.VMEM((depth, width), bf16),
            pltpu.VMEM((depth, width), bf16),
            dma((6,)), dma((2,)), dma((2,)), dma((1,)), dma((1,)), dma((2,)), dma((2,)),
            dma((3,)), dma((3,)), dma((n,)), dma((n,)), dma((n,)), dma((n,)),
            dma((4,)), dma((n,)),
        ],
        compiler_params=pltpu.CompilerParams(
            collective_id=0, has_side_effects=True, vmem_limit_bytes=60 * 2**20
        ),
    )(
        cheb_num, cheb_den, token_ids.reshape(1, tokens), hidden, cotangent,
        w_in[0, 0], w_out, tracker[0, 0], grad_old[0, 0],
    )
    return new_params[None, None], new_tracker[None, None]


def solution(mesh):
    n, groups = mesh.shape["blk"], mesh.shape["grp"]
    fused = 2 < n <= 2 * ROUNDS and groups == 4
    placed = (
        P(("blk", "grp"), None),
        P(("blk", "grp"), None),
        P(("blk", "grp")),
        P("blk", "grp", None, None),
        P(),
        P("blk", "grp", None, None),
        P("blk", "grp", None, None),
        P(),
        P(),
    )
    return jax.shard_map(
        fused_shards if fused else shards,
        mesh=mesh,
        in_specs=placed,
        out_specs=(P("blk", "grp", None, None), P("blk", "grp", None, None)),
        check_vma=False,
    )
```

```python
import functools
import math

import jax
import jax.numpy as jnp
from jax import lax
from jax.experimental import pallas as pl
from jax.experimental.pallas import tpu as pltpu
from jax.sharding import PartitionSpec as P

ROUNDS = 4


epsilon = 1e-06
step_size = 0.25
tanh_scale = math.sqrt(2.0 / math.pi)


def padded(cells, sides, width):
    for axis, dim in sides:
        count = lax.axis_size(axis)
        head = lax.slice_in_dim(cells, 0, width, axis=dim)
        tail = lax.slice_in_dim(cells, cells.shape[dim] - width, cells.shape[dim], axis=dim)
        cells = jnp.concatenate(
            [
                lax.ppermute(tail, axis, [(i, (i + 1) % count) for i in range(count)]),
                cells,
                lax.ppermute(head, axis, [((i + 1) % count, i) for i in range(count)]),
            ],
            axis=dim,
        )
    return cells


def passed_along(value, axis, by):
    devices = lax.axis_size(axis)
    return lax.ppermute(value, axis, [(i, (i + by) % devices) for i in range(devices)])


def gelu_slope(values):
    cubic = values * values * values
    bent_tanh = jnp.tanh(tanh_scale * (values + 0.044715 * cubic))
    return 0.5 * (1.0 + bent_tanh) + 0.5 * values * (1.0 - bent_tanh * bent_tanh) * tanh_scale * (
        1.0 + 3.0 * 0.044715 * values * values
    )


def cycle_mean(beside_all):
    return ((beside_all[0] + beside_all[1] + beside_all[2]) / 3.0)[None]


def local_grad(hidden, cotangent, token_ids, params, w_out):
    widened = hidden.astype(jnp.float32)
    mean_square = jnp.mean(widened * widened, axis=-1, keepdims=True)
    normed = (widened * lax.rsqrt(mean_square + epsilon)).astype(jnp.bfloat16)
    inv_root = params.shape[0] ** (-0.5)
    pre_act = jnp.dot(normed, params, preferred_element_type=jnp.float32) * inv_root
    masked = jnp.where((token_ids != 0)[:, None], cotangent, jnp.zeros_like(cotangent))
    back_flow = lax.dot_general(
        masked, w_out, (((1,), (1,)), ((), ())), preferred_element_type=jnp.float32
    )
    slope_bf = (back_flow * gelu_slope(pre_act)).astype(jnp.bfloat16)
    return (
        lax.dot_general(
            normed, slope_bf, (((0,), (0,)), ((), ())), preferred_element_type=jnp.float32
        )
        * inv_root
    )


def shards(hidden, cotangent, token_ids, w_in, w_out, tracker, grad_old, cheb_num, cheb_den):
    beside_all = padded(w_in, (("blk", 0),), 1).astype(jnp.float32)
    cycle_mixed = cycle_mean(beside_all)
    groups = lax.axis_size("grp")
    group_sum = lax.psum(cycle_mixed.astype(jnp.bfloat16), "grp").astype(jnp.float32)
    group_avg = group_sum / groups
    new_params = (group_avg - step_size * tracker.astype(jnp.float32)).astype(jnp.bfloat16)
    weights = cheb_num.astype(jnp.float32) / cheb_den.astype(jnp.float32)
    start_iter = tracker.astype(jnp.float32)
    coeffs = jnp.zeros((2 * ROUNDS + 1,), jnp.float32).at[ROUNDS].set(1.0)
    older_coef = coeffs
    current_coef = coeffs
    for turn_idx in range(ROUNDS):
        mixed_coef = (jnp.roll(current_coef, 1) + current_coef + jnp.roll(current_coef, -1)) / 3.0
        next_coef = weights[turn_idx] * mixed_coef + (1.0 - weights[turn_idx]) * older_coef
        older_coef, current_coef = (current_coef, next_coef)
    consensus = current_coef[ROUNDS] * start_iter
    for hop_len in range(1, ROUNDS + 1):
        for direction in (1, -1):
            shifted = passed_along(tracker, "blk", direction * hop_len)
            consensus = consensus + current_coef[ROUNDS + direction * hop_len] * shifted.astype(
                jnp.float32
            )
    grad_new = local_grad(hidden, cotangent, token_ids, new_params[0, 0], w_out)[None, None]
    new_tracker = (consensus + grad_new - grad_old.astype(jnp.float32)).astype(jnp.bfloat16)
    return (new_params, new_tracker)


MESH = pl.DeviceIdType.MESH
f32 = jnp.float32
bf16 = jnp.bfloat16


def cycle_coeffs(num_ref, den_ref, count):
    coef = [1.0] + [0.0] * (ROUNDS + 1)
    older = coef
    for turn in range(ROUNDS):
        omega = jnp.full((1, 128), num_ref[turn], jnp.int32).astype(f32) / jnp.full(
            (1, 128), den_ref[turn], jnp.int32
        ).astype(f32)
        following = []
        for dist in range(ROUNDS + 1):
            mixed = (coef[abs(dist - 1)] + coef[dist] + coef[dist + 1]) / 3.0
            following.append(omega * mixed + (1.0 - omega) * older[dist])
        older, coef = (coef, following + [0.0])
    folded = [None] * count
    for hop in range(-ROUNDS, ROUNDS + 1):
        at = hop % count
        folded[at] = coef[abs(hop)] if folded[at] is None else folded[at] + coef[abs(hop)]
    return folded


def fused_kernel(
    n, groups, tile,
    num_ref, den_ref, ids_ref, hid_ref, cot_ref, win_ref, wout_ref, trk_ref, old_ref,
    par_out, trk_out,
    hid, cot, win, wout, trk, old,
    wout_t, normed, normed_t, back, slope, grad,
    rs_core, rs_send, rs_x, m_own, m_bf, m_recv, mix, params,
    got, cons_send, cons, result,
    load_sem, core_s, core_r, x_s, x_r, nb_s, nb_r, ag_s, ag_r, p1_s, p1_r, p2_s, p2_r,
    po_sem, to_sem,
):
    b = lax.axis_index("blk")
    g = lax.axis_index("grp")
    rows_all, depth = hid.shape
    width = win.shape[1]
    part = width // groups
    chunk = depth // n
    core, side = lax.rem(g, 2), g // 2
    core_peer = side * 2 + (1 - core)
    x_peer = (1 - side) * 2 + core
    diag = (1 - side) * 2 + (1 - core)
    inv_root = depth ** (-0.5)

    def cols(which):
        return pl.ds(pl.multiple_of(which * part, 128), part)

    def rows(which):
        return pl.ds(pl.multiple_of(which * chunk, 16), chunk)

    def ring(by):
        return lax.rem(b + (by + n), n)

    loads = [
        pltpu.make_async_copy(s, d, load_sem.at[i])
        for i, (s, d) in enumerate(
            [(wout_ref, wout), (hid_ref, hid), (cot_ref, cot), (win_ref, win), (trk_ref, trk), (old_ref, old)]
        )
    ]
    for load in loads:
        load.start()

    barrier = pltpu.get_barrier_semaphore()
    for peer in (core_peer, x_peer):
        pl.semaphore_signal(barrier, inc=1, device_id=(b, peer), device_id_type=MESH)
    for by in range(1, n):
        pl.semaphore_signal(barrier, inc=1, device_id=(ring(by), g), device_id_type=MESH)
    pl.semaphore_wait(barrier, n + 1)

    def remote(source, target, send, recv, to):
        return pltpu.make_async_remote_copy(
            src_ref=source, dst_ref=target, send_sem=send, recv_sem=recv,
            device_id=to, device_id_type=MESH,
        )

    to_core = [
        remote(win_ref.at[:, cols(w)], rs_core.at[i], core_s.at[i], core_r.at[i], (b, core_peer))
        for i, w in ((1, diag), (0, core_peer))
    ]
    for copy in to_core:
        copy.start()
    first = {
        by: remote(
            trk_ref.at[rows(ring(by))], got.at[by], p1_s.at[by], p1_r.at[by], (ring(by), g)
        )
        for by in range(1, n)
    }
    order = sorted(range(1, n), key=lambda by: -min(by, n - by))
    for by in order[:3]:
        first[by].start()

    loads[0].wait()
    wout_t[...] = wout[...].T
    loads[2].wait()

    def flow(i, carry):
        at = pl.ds(pl.multiple_of(i * tile, tile), tile)
        back[at, :] = jnp.dot(cot[at, :], wout_t[...], preferred_element_type=f32)
        return carry

    loads[1].wait()

    def norm(i, carry):
        at = pl.ds(pl.multiple_of(i * tile, tile), tile)
        wide = hid[at, :].astype(f32)
        mean_square = jnp.mean(wide * wide, axis=-1, keepdims=True)
        scaled = (wide * lax.rsqrt(mean_square + epsilon)).astype(bf16)
        normed[at, :] = scaled
        flipped = scaled.astype(f32).T
        normed_t[:, at] = jnp.where(ids_ref[:, at] != 0, flipped, 0.0).astype(bf16)
        return carry

    loads[3].wait()
    for copy in to_core:
        copy.wait()
    rs_send[...] = (win[:, cols(x_peer)].astype(f32) + rs_core[1].astype(f32)).astype(bf16)
    to_x = remote(rs_send, rs_x, x_s.at[0], x_r.at[0], (b, x_peer))
    to_x.start()
    m_own[...] = win[:, cols(g)].astype(f32) + rs_core[0].astype(f32)
    lax.fori_loop(0, rows_all // tile, norm, 0)
    to_x.wait()
    m_own[...] += rs_x[...].astype(f32)
    m_bf[...] = m_own[...].astype(bf16)
    beside = [
        remote(m_bf, m_recv.at[i], nb_s.at[i], nb_r.at[i], (ring(by), g))
        for i, by in ((0, 1), (1, -1))
    ]
    for copy in beside:
        copy.start()
    for by in order[3:]:
        first[by].start()

    loads[4].wait()
    loads[5].wait()
    for by in order:
        first[by].wait()
    got[0] = trk[rows(b), :]
    coef = cycle_coeffs(num_ref, den_ref, n)
    lanes = coef[0].shape[1]

    def combine(i, carry):
        at = pl.ds(pl.multiple_of(i * lanes, lanes), lanes)
        parts = [got[by, :, at].astype(f32) for by in range(n)]
        for to in range(n):
            total = coef[to] * parts[0]
            for by in range(1, n):
                total = total + coef[(to + by) % n] * parts[by]
            if to == 0:
                cons[rows(b), at] = total.astype(bf16)
            else:
                cons_send[to, :, at] = total.astype(bf16)
        return carry

    lax.fori_loop(0, width // lanes, combine, 0)
    second = {
        by: remote(cons_send.at[by], cons.at[rows(b)], p2_s.at[by], p2_r.at[by], (ring(by), g))
        for by in range(1, n)
    }
    for by in order:
        second[by].start()
    lax.fori_loop(0, rows_all // tile, flow, 0)

    for copy in beside:
        copy.wait()
    mix[0] = (
        (m_own[...] + m_recv[0].astype(f32) + m_recv[1].astype(f32)) / (3.0 * groups)
    ).astype(bf16)
    gather = [
        remote(mix.at[0], mix.at[1], ag_s.at[0], ag_r.at[0], (b, x_peer)),
        remote(mix.at[0], mix.at[2], ag_s.at[1], ag_r.at[1], (b, core_peer)),
        remote(mix.at[1], mix.at[3], ag_s.at[2], ag_r.at[2], (b, core_peer)),
    ]
    gather[0].start()
    gather[1].start()

    written = []
    for slot, owner in ((0, g), (2, core_peer), (1, x_peer), (3, diag)):
        if slot == 2:
            gather[1].wait()
        if slot == 1:
            gather[0].wait()
            gather[2].start()
        if slot == 3:
            gather[2].wait()
        here = cols(owner)
        params[slot] = (
            mix[slot].astype(f32) - step_size * trk[:, here].astype(f32)
        ).astype(bf16)
        copy = pltpu.make_async_copy(params.at[slot], par_out.at[:, here], po_sem.at[slot])
        copy.start()
        written.append(copy)

        def tokens(i, carry, slot=slot, here=here):
            at = pl.ds(pl.multiple_of(i * tile, tile), tile)
            p = jnp.dot(normed[at, :], params[slot], preferred_element_type=f32) * inv_root
            square = p * p
            bent = jnp.tanh(p * (tanh_scale + (tanh_scale * 0.044715) * square))
            ramp = p * (tanh_scale + (3.0 * 0.044715 * tanh_scale) * square)
            bend = (1.0 + bent) * (1.0 + (1.0 - bent) * ramp)
            slope[at, :] = (back[at, here] * (0.5 * bend)).astype(bf16)
            return carry

        lax.fori_loop(0, rows_all // tile, tokens, 0)
        grad[:, here] = (
            jnp.dot(normed_t[...], slope[...], preferred_element_type=f32) * inv_root
            - old[:, here].astype(f32)
        )

    for by in [0] + order:
        if by:
            second[by].wait()
        here = rows(ring(-by))
        result[here, :] = (grad[here, :] + cons[here, :].astype(f32)).astype(bf16)
        copy = pltpu.make_async_copy(result.at[here], trk_out.at[here], to_sem.at[by])
        copy.start()
        written.append(copy)
    for copy in written:
        copy.wait()


def fused_shards(hidden, cotangent, token_ids, w_in, w_out, tracker, grad_old, cheb_num, cheb_den):
    n, groups = lax.axis_size("blk"), lax.axis_size("grp")
    tokens, depth = hidden.shape
    width = w_in.shape[-1]
    part, chunk = width // groups, depth // n
    tile = 256
    leaf = jax.ShapeDtypeStruct((depth, width), bf16)
    hbm, smem, vmem = (
        pl.BlockSpec(memory_space=space) for space in (pl.ANY, pltpu.SMEM, pltpu.VMEM)
    )
    dma = pltpu.SemaphoreType.DMA
    new_params, new_tracker = pl.pallas_call(
        functools.partial(fused_kernel, n, groups, tile),
        out_shape=(leaf, leaf),
        in_specs=[smem, smem, vmem] + [hbm] * 6,
        out_specs=(hbm, hbm),
        scratch_shapes=[
            pltpu.VMEM((tokens, depth), bf16),
            pltpu.VMEM((tokens, depth), bf16),
            pltpu.VMEM((depth, width), bf16),
            pltpu.VMEM((width, depth), bf16),
            pltpu.VMEM((depth, width), bf16),
            pltpu.VMEM((depth, width), bf16),
            pltpu.VMEM((depth, width), bf16),
            pltpu.VMEM((tokens, depth), bf16),
            pltpu.VMEM((depth, tokens), bf16),
            pltpu.VMEM((tokens, width), f32),
            pltpu.VMEM((tokens, part), bf16),
            pltpu.VMEM((depth, width), f32),
            pltpu.VMEM((2, depth, part), bf16),
            pltpu.VMEM((depth, part), bf16),
            pltpu.VMEM((depth, part), bf16),
            pltpu.VMEM((depth, part), f32),
            pltpu.VMEM((depth, part), bf16),
            pltpu.VMEM((2, depth, part), bf16),
            pltpu.VMEM((4, depth, part), bf16),
            pltpu.VMEM((4, depth, part), bf16),
            pltpu.VMEM((n, chunk, width), bf16),
            pltpu.VMEM((n, chunk, width), bf16),
            pltpu.VMEM((depth, width), bf16),
            pltpu.VMEM((depth, width), bf16),
            dma((6,)), dma((2,)), dma((2,)), dma((1,)), dma((1,)), dma((2,)), dma((2,)),
            dma((3,)), dma((3,)), dma((n,)), dma((n,)), dma((n,)), dma((n,)),
            dma((4,)), dma((n,)),
        ],
        compiler_params=pltpu.CompilerParams(
            collective_id=0, has_side_effects=True, vmem_limit_bytes=60 * 2**20
        ),
    )(
        cheb_num, cheb_den, token_ids.reshape(1, tokens), hidden, cotangent,
        w_in[0, 0], w_out, tracker[0, 0], grad_old[0, 0],
    )
    return new_params[None, None], new_tracker[None, None]


def solution(mesh):
    n, groups = mesh.shape["blk"], mesh.shape["grp"]
    fused = 2 < n <= 2 * ROUNDS and groups == 4
    placed = (
        P(("blk", "grp"), None),
        P(("blk", "grp"), None),
        P(("blk", "grp")),
        P("blk", "grp", None, None),
        P(),
        P("blk", "grp", None, None),
        P("blk", "grp", None, None),
        P(),
        P(),
    )
    return jax.shard_map(
        fused_shards if fused else shards,
        mesh=mesh,
        in_specs=placed,
        out_specs=(P("blk", "grp", None, None), P("blk", "grp", None, None)),
        check_vma=False,
    )
```

```python
import functools
import math

import jax
import jax.numpy as jnp
from jax import lax
from jax.experimental import pallas as pl
from jax.experimental.pallas import tpu as pltpu
from jax.sharding import PartitionSpec as P

ROUNDS = 4


epsilon = 1e-06
step_size = 0.25
tanh_scale = math.sqrt(2.0 / math.pi)


def padded(cells, sides, width):
    for axis, dim in sides:
        count = lax.axis_size(axis)
        head = lax.slice_in_dim(cells, 0, width, axis=dim)
        tail = lax.slice_in_dim(cells, cells.shape[dim] - width, cells.shape[dim], axis=dim)
        cells = jnp.concatenate(
            [
                lax.ppermute(tail, axis, [(i, (i + 1) % count) for i in range(count)]),
                cells,
                lax.ppermute(head, axis, [((i + 1) % count, i) for i in range(count)]),
            ],
            axis=dim,
        )
    return cells


def passed_along(value, axis, by):
    devices = lax.axis_size(axis)
    return lax.ppermute(value, axis, [(i, (i + by) % devices) for i in range(devices)])


def gelu_slope(values):
    cubic = values * values * values
    bent_tanh = jnp.tanh(tanh_scale * (values + 0.044715 * cubic))
    return 0.5 * (1.0 + bent_tanh) + 0.5 * values * (1.0 - bent_tanh * bent_tanh) * tanh_scale * (
        1.0 + 3.0 * 0.044715 * values * values
    )


def cycle_mean(beside_all):
    return ((beside_all[0] + beside_all[1] + beside_all[2]) / 3.0)[None]


def local_grad(hidden, cotangent, token_ids, params, w_out):
    widened = hidden.astype(jnp.float32)
    mean_square = jnp.mean(widened * widened, axis=-1, keepdims=True)
    normed = (widened * lax.rsqrt(mean_square + epsilon)).astype(jnp.bfloat16)
    inv_root = params.shape[0] ** (-0.5)
    pre_act = jnp.dot(normed, params, preferred_element_type=jnp.float32) * inv_root
    masked = jnp.where((token_ids != 0)[:, None], cotangent, jnp.zeros_like(cotangent))
    back_flow = lax.dot_general(
        masked, w_out, (((1,), (1,)), ((), ())), preferred_element_type=jnp.float32
    )
    slope_bf = (back_flow * gelu_slope(pre_act)).astype(jnp.bfloat16)
    return (
        lax.dot_general(
            normed, slope_bf, (((0,), (0,)), ((), ())), preferred_element_type=jnp.float32
        )
        * inv_root
    )


def shards(hidden, cotangent, token_ids, w_in, w_out, tracker, grad_old, cheb_num, cheb_den):
    beside_all = padded(w_in, (("blk", 0),), 1).astype(jnp.float32)
    cycle_mixed = cycle_mean(beside_all)
    groups = lax.axis_size("grp")
    group_sum = lax.psum(cycle_mixed.astype(jnp.bfloat16), "grp").astype(jnp.float32)
    group_avg = group_sum / groups
    new_params = (group_avg - step_size * tracker.astype(jnp.float32)).astype(jnp.bfloat16)
    weights = cheb_num.astype(jnp.float32) / cheb_den.astype(jnp.float32)
    start_iter = tracker.astype(jnp.float32)
    coeffs = jnp.zeros((2 * ROUNDS + 1,), jnp.float32).at[ROUNDS].set(1.0)
    older_coef = coeffs
    current_coef = coeffs
    for turn_idx in range(ROUNDS):
        mixed_coef = (jnp.roll(current_coef, 1) + current_coef + jnp.roll(current_coef, -1)) / 3.0
        next_coef = weights[turn_idx] * mixed_coef + (1.0 - weights[turn_idx]) * older_coef
        older_coef, current_coef = (current_coef, next_coef)
    consensus = current_coef[ROUNDS] * start_iter
    for hop_len in range(1, ROUNDS + 1):
        for direction in (1, -1):
            shifted = passed_along(tracker, "blk", direction * hop_len)
            consensus = consensus + current_coef[ROUNDS + direction * hop_len] * shifted.astype(
                jnp.float32
            )
    grad_new = local_grad(hidden, cotangent, token_ids, new_params[0, 0], w_out)[None, None]
    new_tracker = (consensus + grad_new - grad_old.astype(jnp.float32)).astype(jnp.bfloat16)
    return (new_params, new_tracker)


MESH = pl.DeviceIdType.MESH
f32 = jnp.float32
bf16 = jnp.bfloat16


def cycle_coeffs(num_ref, den_ref, count):
    coef = [1.0] + [0.0] * (ROUNDS + 1)
    older = coef
    for turn in range(ROUNDS):
        omega = jnp.full((1, 128), num_ref[turn], jnp.int32).astype(f32) / jnp.full(
            (1, 128), den_ref[turn], jnp.int32
        ).astype(f32)
        following = []
        for dist in range(ROUNDS + 1):
            mixed = (coef[abs(dist - 1)] + coef[dist] + coef[dist + 1]) / 3.0
            following.append(omega * mixed + (1.0 - omega) * older[dist])
        older, coef = (coef, following + [0.0])
    folded = [None] * count
    for hop in range(-ROUNDS, ROUNDS + 1):
        at = hop % count
        folded[at] = coef[abs(hop)] if folded[at] is None else folded[at] + coef[abs(hop)]
    return folded


def fused_kernel(
    n, groups, tile,
    num_ref, den_ref, ids_ref, hid_ref, cot_ref, win_ref, wout_ref, trk_ref, old_ref,
    par_out, trk_out,
    hid, cot, win, wout, trk, old,
    wout_t, normed, normed_t, back, slope, grad,
    rs_core, rs_send, rs_x, m_own, m_bf, m_recv, mix, params,
    got, cons_send, cons, result,
    load_sem, core_s, core_r, x_s, x_r, nb_s, nb_r, ag_s, ag_r, p1_s, p1_r, p2_s, p2_r,
    po_sem, to_sem,
):
    b = lax.axis_index("blk")
    g = lax.axis_index("grp")
    rows_all, depth = hid.shape
    width = win.shape[1]
    part = width // groups
    chunk = depth // n
    core, side = lax.rem(g, 2), g // 2
    core_peer = side * 2 + (1 - core)
    x_peer = (1 - side) * 2 + core
    diag = (1 - side) * 2 + (1 - core)
    inv_root = depth ** (-0.5)

    def cols(which):
        return pl.ds(pl.multiple_of(which * part, 128), part)

    def rows(which):
        return pl.ds(pl.multiple_of(which * chunk, 16), chunk)

    def ring(by):
        return lax.rem(b + (by + n), n)

    loads = [
        pltpu.make_async_copy(s, d, load_sem.at[i])
        for i, (s, d) in enumerate(
            [(wout_ref, wout), (hid_ref, hid), (cot_ref, cot), (win_ref, win), (trk_ref, trk), (old_ref, old)]
        )
    ]
    for load in loads:
        load.start()

    barrier = pltpu.get_barrier_semaphore()
    for peer in (core_peer, x_peer):
        pl.semaphore_signal(barrier, inc=1, device_id=(b, peer), device_id_type=MESH)
    for by in range(1, n):
        pl.semaphore_signal(barrier, inc=1, device_id=(ring(by), g), device_id_type=MESH)
    pl.semaphore_wait(barrier, n + 1)

    def remote(source, target, send, recv, to):
        return pltpu.make_async_remote_copy(
            src_ref=source, dst_ref=target, send_sem=send, recv_sem=recv,
            device_id=to, device_id_type=MESH,
        )

    to_core = [
        remote(win_ref.at[:, cols(w)], rs_core.at[i], core_s.at[i], core_r.at[i], (b, core_peer))
        for i, w in ((1, diag), (0, core_peer))
    ]
    for copy in to_core:
        copy.start()
    first = {
        by: remote(
            trk_ref.at[rows(ring(by))], got.at[by], p1_s.at[by], p1_r.at[by], (ring(by), g)
        )
        for by in range(1, n)
    }
    order = sorted(range(1, n), key=lambda by: -min(by, n - by))
    for by in order[:3]:
        first[by].start()

    loads[0].wait()
    wout_t[...] = wout[...].T
    loads[2].wait()

    def flow(i, carry):
        at = pl.ds(pl.multiple_of(i * tile, tile), tile)
        back[at, :] = jnp.dot(cot[at, :], wout_t[...], preferred_element_type=f32)
        return carry

    loads[1].wait()

    def norm(i, carry):
        at = pl.ds(pl.multiple_of(i * tile, tile), tile)
        wide = hid[at, :].astype(f32)
        mean_square = jnp.mean(wide * wide, axis=-1, keepdims=True)
        scaled = (wide * lax.rsqrt(mean_square + epsilon)).astype(bf16)
        normed[at, :] = scaled
        flipped = scaled.astype(f32).T
        normed_t[:, at] = jnp.where(ids_ref[:, at] != 0, flipped, 0.0).astype(bf16)
        return carry

    loads[3].wait()
    for copy in to_core:
        copy.wait()
    rs_send[...] = (win[:, cols(x_peer)].astype(f32) + rs_core[1].astype(f32)).astype(bf16)
    to_x = remote(rs_send, rs_x, x_s.at[0], x_r.at[0], (b, x_peer))
    to_x.start()
    m_own[...] = win[:, cols(g)].astype(f32) + rs_core[0].astype(f32)
    lax.fori_loop(0, rows_all // tile, norm, 0)
    to_x.wait()
    m_own[...] += rs_x[...].astype(f32)
    m_bf[...] = m_own[...].astype(bf16)
    beside = [
        remote(m_bf, m_recv.at[i], nb_s.at[i], nb_r.at[i], (ring(by), g))
        for i, by in ((0, 1), (1, -1))
    ]
    for copy in beside:
        copy.start()
    for by in order[3:]:
        first[by].start()

    loads[4].wait()
    loads[5].wait()
    for by in order:
        first[by].wait()
    got[0] = trk[rows(b), :]
    coef = cycle_coeffs(num_ref, den_ref, n)
    lanes = coef[0].shape[1]

    def combine(i, carry):
        at = pl.ds(pl.multiple_of(i * lanes, lanes), lanes)
        parts = [got[by, :, at].astype(f32) for by in range(n)]
        for to in range(n):
            total = coef[to] * parts[0]
            for by in range(1, n):
                total = total + coef[(to + by) % n] * parts[by]
            if to == 0:
                cons[rows(b), at] = total.astype(bf16)
            else:
                cons_send[to, :, at] = total.astype(bf16)
        return carry

    lax.fori_loop(0, width // lanes, combine, 0)
    second = {
        by: remote(cons_send.at[by], cons.at[rows(b)], p2_s.at[by], p2_r.at[by], (ring(by), g))
        for by in range(1, n)
    }
    for by in order:
        second[by].start()
    lax.fori_loop(0, rows_all // tile, flow, 0)

    for copy in beside:
        copy.wait()
    mix[0] = (
        (m_own[...] + m_recv[0].astype(f32) + m_recv[1].astype(f32)) / (3.0 * groups)
    ).astype(bf16)
    gather = [
        remote(mix.at[0], mix.at[1], ag_s.at[0], ag_r.at[0], (b, x_peer)),
        remote(mix.at[0], mix.at[2], ag_s.at[1], ag_r.at[1], (b, core_peer)),
        remote(mix.at[1], mix.at[3], ag_s.at[2], ag_r.at[2], (b, core_peer)),
    ]
    gather[0].start()
    gather[1].start()

    written = []
    for slot, owner in ((0, g), (2, core_peer), (1, x_peer), (3, diag)):
        if slot == 2:
            gather[1].wait()
        if slot == 1:
            gather[0].wait()
            gather[2].start()
        if slot == 3:
            gather[2].wait()
        here = cols(owner)
        params[slot] = (
            mix[slot].astype(f32) - step_size * trk[:, here].astype(f32)
        ).astype(bf16)
        copy = pltpu.make_async_copy(params.at[slot], par_out.at[:, here], po_sem.at[slot])
        copy.start()
        written.append(copy)

        def tokens(i, carry, slot=slot, here=here):
            at = pl.ds(pl.multiple_of(i * tile, tile), tile)
            p = jnp.dot(normed[at, :], params[slot], preferred_element_type=f32) * inv_root
            square = p * p
            bent = jnp.tanh(p * (tanh_scale + (tanh_scale * 0.044715) * square))
            ramp = p * (tanh_scale + (3.0 * 0.044715 * tanh_scale) * square)
            bend = (1.0 + bent) * (1.0 + (1.0 - bent) * ramp)
            slope[at, :] = (back[at, here] * (0.5 * bend)).astype(bf16)
            return carry

        lax.fori_loop(0, rows_all // tile, tokens, 0)
        grad[:, here] = (
            jnp.dot(normed_t[...], slope[...], preferred_element_type=f32) * inv_root
            - old[:, here].astype(f32)
        )

    for by in [0] + order:
        if by:
            second[by].wait()
        here = rows(ring(-by))
        result[here, :] = (grad[here, :] + cons[here, :].astype(f32)).astype(bf16)
        copy = pltpu.make_async_copy(result.at[here], trk_out.at[here], to_sem.at[by])
        copy.start()
        written.append(copy)
    for copy in written:
        copy.wait()


def fused_shards(hidden, cotangent, token_ids, w_in, w_out, tracker, grad_old, cheb_num, cheb_den):
    n, groups = lax.axis_size("blk"), lax.axis_size("grp")
    tokens, depth = hidden.shape
    width = w_in.shape[-1]
    part, chunk = width // groups, depth // n
    tile = 512
    leaf = jax.ShapeDtypeStruct((depth, width), bf16)
    hbm, smem, vmem = (
        pl.BlockSpec(memory_space=space) for space in (pl.ANY, pltpu.SMEM, pltpu.VMEM)
    )
    dma = pltpu.SemaphoreType.DMA
    new_params, new_tracker = pl.pallas_call(
        functools.partial(fused_kernel, n, groups, tile),
        out_shape=(leaf, leaf),
        in_specs=[smem, smem, vmem] + [hbm] * 6,
        out_specs=(hbm, hbm),
        scratch_shapes=[
            pltpu.VMEM((tokens, depth), bf16),
            pltpu.VMEM((tokens, depth), bf16),
            pltpu.VMEM((depth, width), bf16),
            pltpu.VMEM((width, depth), bf16),
            pltpu.VMEM((depth, width), bf16),
            pltpu.VMEM((depth, width), bf16),
            pltpu.VMEM((depth, width), bf16),
            pltpu.VMEM((tokens, depth), bf16),
            pltpu.VMEM((depth, tokens), bf16),
            pltpu.VMEM((tokens, width), f32),
            pltpu.VMEM((tokens, part), bf16),
            pltpu.VMEM((depth, width), f32),
            pltpu.VMEM((2, depth, part), bf16),
            pltpu.VMEM((depth, part), bf16),
            pltpu.VMEM((depth, part), bf16),
            pltpu.VMEM((depth, part), f32),
            pltpu.VMEM((depth, part), bf16),
            pltpu.VMEM((2, depth, part), bf16),
            pltpu.VMEM((4, depth, part), bf16),
            pltpu.VMEM((4, depth, part), bf16),
            pltpu.VMEM((n, chunk, width), bf16),
            pltpu.VMEM((n, chunk, width), bf16),
            pltpu.VMEM((depth, width), bf16),
            pltpu.VMEM((depth, width), bf16),
            dma((6,)), dma((2,)), dma((2,)), dma((1,)), dma((1,)), dma((2,)), dma((2,)),
            dma((3,)), dma((3,)), dma((n,)), dma((n,)), dma((n,)), dma((n,)),
            dma((4,)), dma((n,)),
        ],
        compiler_params=pltpu.CompilerParams(
            collective_id=0, has_side_effects=True, vmem_limit_bytes=60 * 2**20
        ),
    )(
        cheb_num, cheb_den, token_ids.reshape(1, tokens), hidden, cotangent,
        w_in[0, 0], w_out, tracker[0, 0], grad_old[0, 0],
    )
    return new_params[None, None], new_tracker[None, None]


def solution(mesh):
    n, groups = mesh.shape["blk"], mesh.shape["grp"]
    fused = 2 < n <= 2 * ROUNDS and groups == 4
    placed = (
        P(("blk", "grp"), None),
        P(("blk", "grp"), None),
        P(("blk", "grp")),
        P("blk", "grp", None, None),
        P(),
        P("blk", "grp", None, None),
        P("blk", "grp", None, None),
        P(),
        P(),
    )
    return jax.shard_map(
        fused_shards if fused else shards,
        mesh=mesh,
        in_specs=placed,
        out_specs=(P("blk", "grp", None, None), P("blk", "grp", None, None)),
        check_vma=False,
    )
```
